128 devices in a mesh: mem: 8 (over z_lo, y), sp: 16 (over z_hi, x, core).
Axes of the slice: x: 4, y: 4, z: 4 (z_hi: 2, z_lo: 2; z = z_hi * 2 + z_lo), core: 2. Of those that a mesh axis runs over, the one named last changes fastest.
Arguments:
- anomalies: float32 [64, 3, 256, 4096], P('mem', None, 'sp'), may hold values from -6 to 6
- mean_state: float32 [3, 256, 4096], P(None, 'sp'), may hold values from -3 to 3
- weights: float32 [64], replicated, may hold values from -0.4375 to 0.4375
- station_row: int32 [4096], P('sp'), may hold values from 0 to 14
- station_col: int32 [4096], P('sp'), may hold values from 0 to 4095
- stencil_row: int32 [4, 4096], P(None, 'sp'), may hold values from 0 to 1
- stencil_col: int32 [4, 4096], P(None, 'sp'), may hold values from -1 to 1
- obs_weight: float32 [4, 4096], P(None, 'sp'), may hold values from 0.05 to 0.25
- obs_value: float32 [4, 4096], P(None, 'sp'), may hold values from -6 to 6
- obs_var: float32 [4, 4096], P(None, 'sp'), may hold values from 1 to 10
Outputs:
- obs_anom: float32 [64, 4, 4096], P('mem', None, 'sp')
- gradient: float32 [64], replicated
- hessian: float32 [64, 64], replicated
The draws below stay inside these ranges and needn't reach their ends.
All inputs are finite; a program needn't handle non-finite values.
Results may differ from the reference program's by a relative error of at most 0.0003.
Values sent between devices are 32-bit elements; how exact they have to be, the bound alone decides.
No kernel may reach another device: no remote copies, remote signals or barrier semaphores. Data moves between devices by JAX's collectives and lax.ppermute only.
A program may use at most 192 MiB of HBM per device.

```python
import math
import jax
import jax.numpy as jnp
from jax import lax

M = 64
STEPS = 4
TX = 16
NY = 4096
STA_DEV = 256
NX = 256
STATIONS = 4096


def with_ends(array, rng, least, top_value):
    place = [jax.random.randint(jax.random.fold_in(rng, axis), (), 0, length) for axis, length in enumerate(array.shape)]
    widest = array.shape.index(max(array.shape))
    next_to = place[:widest] + [(place[widest] + 1) % array.shape[widest]] + place[widest + 1:]
    return array.at[tuple(place)].set(least).at[tuple(next_to)].set(top_value)


def shard_levels(key, shape, pieces, least, top_value):
    loudness, own = 1.0, jax.random.fold_in(key, 6)
    for position, parts in pieces:
        draws = jnp.exp(jax.random.uniform(jax.random.fold_in(own, position), (parts,), jnp.float32, least / len(pieces), top_value / len(pieces)))
        loudness = loudness * jnp.repeat(draws, shape[position] // parts).reshape([-1 if axis == position else 1 for axis in range(len(shape))])
    return loudness


def scatter_about(rng, shape, spread, most, cuts=(), held_as=jnp.bfloat16):
    array = spread * jax.random.normal(rng, shape, jnp.float32)
    if cuts:
        array = array * shard_levels(rng, shape, cuts, -0.22, 0.18)
    return jnp.clip(array, -most, most).astype(held_as)


def setup_inputs(seed: int = 0) -> dict:
    keys = jax.random.split(jax.random.key(seed), 11)
    anomalies = scatter_about(keys[0], (M, 3, NX, NY), 1.0, 6.0, ((0, 8), (2, 16)), jnp.float32)
    mean_state = scatter_about(keys[1], (3, NX, NY), 0.2, 3.0, ((1, 16),), jnp.float32)
    weights = scatter_about(keys[2], (M,), 0.03, 0.4375, (), jnp.float32)
    station_row = with_ends(jax.random.randint(keys[3], (STATIONS,), 0, TX - 1), jax.random.fold_in(keys[3], 1), 0, (TX - 1) - 1).astype(jnp.int32)
    station_col = with_ends(jax.random.randint(keys[4], (STATIONS,), 0, NY), jax.random.fold_in(keys[4], 1), 0, NY - 1).astype(jnp.int32)
    stencil_row = with_ends(jax.random.randint(keys[5], (4, STATIONS), 0, 2), jax.random.fold_in(keys[5], 1), 0, 1).astype(jnp.int32)
    stencil_col = with_ends(jax.random.randint(keys[6], (4, STATIONS), -1, 2), jax.random.fold_in(keys[6], 1), -1, 1).astype(jnp.int32)
    obs_weight = jnp.clip(0.05 + 0.2 * jax.random.uniform(keys[7], (4, STATIONS), jnp.float32) ** shard_levels(keys[7], (4, STATIONS), ((1, 16),), -0.2, 0.2), 0.05, 0.25)
    obs_value = scatter_about(keys[8], (STEPS, STATIONS), 0.5, 6.0, ((1, 16),), jnp.float32)
    obs_var = jnp.clip(jnp.exp(math.log(10.0) - 2.3025851 * jax.random.uniform(keys[9], (STEPS, STATIONS), jnp.float32) ** shard_levels(keys[9], (STEPS, STATIONS), ((1, 16),), -0.2, 0.2)), 1.0, 10.0)
    return dict(anomalies=anomalies, mean_state=mean_state, weights=weights, station_row=station_row, station_col=station_col, stencil_row=stencil_row, stencil_col=stencil_col, obs_weight=obs_weight, obs_value=obs_value, obs_var=obs_var)


time_step = 1.0
coriolis = 0.1
perturb = 0.1


def row_diff(a):
    return (jnp.roll(a, -1, axis=-2) - jnp.roll(a, 1, axis=-2)) * 0.5


def col_diff(a):
    return (jnp.roll(a, -1, axis=-1) - jnp.roll(a, 1, axis=-1)) * 0.5


def model_step(state):
    height, along, across = state[0], state[1], state[2]
    depth = 1.0 + height
    fresh = height - time_step * (row_diff(depth * along) + col_diff(depth * across))
    new_u = along + time_step * (coriolis * across - row_diff(fresh) - along * row_diff(along) - across * col_diff(along))
    new_v = across + time_step * (-coriolis * along - col_diff(fresh) - along * row_diff(across) - across * col_diff(across))
    return jnp.stack([fresh, new_u, new_v])


def reference(anomalies, mean_state, weights, station_row, station_col, stencil_row, stencil_col, obs_weight, obs_value, obs_var):
    increment = jnp.tensordot(weights, anomalies, axes=1, precision=lax.Precision.HIGHEST)
    centre = mean_state + increment
    strip = (jnp.arange(STATIONS, dtype=jnp.int32) // STA_DEV).astype(jnp.int32)
    rows = strip[None, :] * TX + station_row[None, :] + stencil_row
    cols = (station_col[None, :] + stencil_col) % NY
    flat_index = (rows * NY + cols).astype(jnp.int32)

    def run_member(anomaly):
        state = centre + perturb * anomaly
        seen = []
        for step in range(STEPS):
            state = model_step(state)
            picked = state[0].reshape(-1)[flat_index]
            seen.append(jnp.sum(obs_weight * picked, axis=0))
        return jnp.stack(seen)

    observed = lax.map(run_member, anomalies)
    mean_obs = jnp.mean(observed, axis=0)
    obs_anom = (observed - mean_obs) / perturb
    flat_anom = obs_anom.reshape(M, -1)
    weighted = flat_anom * (1.0 / obs_var).reshape(-1)
    innov = (obs_value - mean_obs).reshape(-1)
    gram = jnp.dot(weighted, flat_anom.T, precision=lax.Precision.HIGHEST)
    pull = jnp.dot(weighted, innov, precision=lax.Precision.HIGHEST)
    hessian = gram + (M - 1) * jnp.eye(M, dtype=jnp.float32)
    gradient = (M - 1) * weights - pull
    return obs_anom, gradient, hessian
```

```python
import jax
import jax.numpy as jnp
from jax import lax
from jax.experimental import pallas as pl
from jax.experimental.pallas import tpu as pltpu
from jax.sharding import PartitionSpec as P

STEPS = 4
HALO = 2 * STEPS - 1
LANES = 128

time_step = 1.0
coriolis = 0.1
perturb = 0.1


def ring(axis, step):
    count = lax.axis_size(axis)
    return [(i, (i + step) % count) for i in range(count)]


def prepare_kernel(place, weights, anom, turned, top, bottom, partial):
    members, rows = anom.shape[0], anom.shape[2]
    chunks, width = partial.shape[0], partial.shape[3]
    first = place[0] * members
    scales = [weights[first + m] for m in range(members)]

    def column(t, carry):
        at = pl.ds(pl.multiple_of(t * LANES, LANES), LANES)
        block = anom[:, 0, :, at]
        turned[0, :, :, at] = jnp.swapaxes(block, 0, 1)
        total = scales[0] * block[0]
        for m in range(1, members):
            total = total + scales[m] * block[m]
        per = width // LANES
        inner = pl.ds(pl.multiple_of((t % per) * LANES, LANES), LANES)
        partial[t // per, 0, :, inner] = total
        return carry

    lax.fori_loop(0, anom.shape[3] // LANES, column, 0)

    @pl.when(pl.program_id(1) == 0)
    def _():
        top[0] = turned[0, :HALO]

    @pl.when(pl.program_id(1) == 1)
    def _():
        bottom[0] = turned[0, rows - HALO :]


def prepare(place, weights, anomalies):
    members, fields, rows, columns = anomalies.shape
    half = rows // 2
    chunks = lax.axis_size("mem")
    width = columns // chunks
    smem = pl.BlockSpec(memory_space=pltpu.SMEM)
    edge = pl.BlockSpec((1, HALO, members, columns), lambda f, r: (f, 0, 0, 0))
    return pl.pallas_call(
        prepare_kernel,
        grid=(fields, 2),
        in_specs=[smem, smem, pl.BlockSpec((members, 1, half, columns), lambda f, r: (0, f, r, 0))],
        out_specs=[
            pl.BlockSpec((1, half, members, columns), lambda f, r: (f, r, 0, 0)),
            edge,
            edge,
            pl.BlockSpec((chunks, 1, half, width), lambda f, r: (0, f, r, 0)),
        ],
        out_shape=[
            jax.ShapeDtypeStruct((fields, rows, members, columns), jnp.float32),
            jax.ShapeDtypeStruct((fields, HALO, members, columns), jnp.float32),
            jax.ShapeDtypeStruct((fields, HALO, members, columns), jnp.float32),
            jax.ShapeDtypeStruct((chunks, fields, rows, width), jnp.float32),
        ],
        compiler_params=pltpu.CompilerParams(vmem_limit_bytes=40 << 20),
        name="prepare",
    )(place, weights, anomalies)


def model_kernel(
    spots, turns, low_c, centre, high_c, obs_weight, own, low, high, out, state, heights, spare, sems
):
    rows, columns = own.shape[1], own.shape[3]
    tiles = columns // LANES
    tall = rows + 2 * HALO
    copies = [
        pltpu.make_async_copy(low, state.at[:, pl.ds(0, HALO)], sems.at[0]),
        pltpu.make_async_copy(own, state.at[:, pl.ds(HALO, rows)], sems.at[1]),
        pltpu.make_async_copy(high, state.at[:, pl.ds(HALO + rows, HALO)], sems.at[2]),
    ]
    for copy in copies:
        copy.start()
    for copy in copies:
        copy.wait()

    lane = lax.broadcasted_iota(jnp.int32, (8, LANES), 1)
    is_first = lane == 0
    is_last = lane == LANES - 1
    chunk_width = centre.shape[3]
    per = chunk_width // LANES

    def begin(i, carry):
        f = i // tiles
        t = i % tiles
        at = pl.ds(pl.multiple_of(t * LANES, LANES), LANES)
        chunk = t // per
        inner = pl.ds(pl.multiple_of((t % per) * LANES, LANES), LANES)
        for r in range(tall):
            if r < HALO:
                base = low_c[chunk, f, pl.ds(low_c.shape[2] - HALO + r, 1), inner]
            elif r < HALO + rows:
                base = centre[chunk, f, pl.ds(r - HALO, 1), inner]
            else:
                base = high_c[chunk, f, pl.ds(r - HALO - rows, 1), inner]
            state[f, r, :, at] = base + perturb * state[f, r, :, at]
        return carry

    lax.fori_loop(0, 3 * tiles, begin, 0)

    def cut(t):
        return pl.ds((t % tiles) * LANES, LANES)

    def shifted(pieces):
        left = [pltpu.roll(p, LANES - 1, 1) for p in pieces]
        right = [pltpu.roll(p, 1, 1) for p in pieces]
        return left, right

    def spread(left, right, t):
        nxt = jnp.where(is_last, left[(t + 1) % tiles], left[t])
        prv = jnp.where(is_first, right[(t - 1) % tiles], right[t])
        return nxt - prv

    def height_row(h, u, v, hn, r):
        flow = [(1.0 + h(r, t)) * v(r, t) for t in range(tiles)]
        left, right = shifted(flow)
        for t in range(tiles):
            below = (1.0 + h(r + 1, t)) * u(r + 1, t)
            above = (1.0 + h(r - 1, t)) * u(r - 1, t)
            hn(r, t, h(r, t) - (0.5 * time_step) * ((below - above) + spread(left, right, t)))

    def momentum_row(h, u, v, un, vn, r):
        hl, hr = shifted([h(r, t) for t in range(tiles)])
        ul, ur = shifted([u(r, t) for t in range(tiles)])
        vl, vr = shifted([v(r, t) for t in range(tiles)])
        for t in range(tiles):
            cu, cv = u(r, t), v(r, t)
            du = (h(r + 1, t) - h(r - 1, t)) + cu * (u(r + 1, t) - u(r - 1, t)) + cv * spread(ul, ur, t)
            dv = spread(hl, hr, t) + cu * (v(r + 1, t) - v(r - 1, t)) + cv * spread(vl, vr, t)
            un(r, t, cu + (time_step * coriolis) * cv - (0.5 * time_step) * du)
            vn(r, t, cv - (time_step * coriolis) * cu - (0.5 * time_step) * dv)

    def reader(ref, *lead):
        return lambda r, t: ref[(*lead, r, slice(None), cut(t))]

    def writer(ref, *lead):
        def put(r, t, value):
            ref[(*lead, r, slice(None), cut(t))] = value

        return put

    h = (state, 0)
    pairs = [((state, 1), (state, 2)), ((spare, 0), (spare, 1))]
    for step in range(STEPS):
        (u, v), (un, vn) = pairs[step % 2], pairs[1 - step % 2]
        low_row = 2 * step + 1
        fresh = (heights, step)

        def height_body(r, carry):
            height_row(reader(*h), reader(*u), reader(*v), writer(*fresh), r)
            return carry

        lax.fori_loop(low_row, tall - low_row, height_body, 0)
        if step + 1 < STEPS:

            def momentum_body(r, carry):
                momentum_row(reader(*fresh), reader(*u), reader(*v), writer(*un), writer(*vn), r)
                return carry

            lax.fori_loop(low_row + 1, tall - low_row - 1, momentum_body, 0)
        h = fresh

    points = obs_weight.shape[0]
    stations = obs_weight.shape[1]
    for group in range(stations // LANES):

        def pick(s, held):
            here = lane == s
            fresh_held = list(held)
            for k in range(points):
                spot = spots[k, group * LANES + s]
                turn = turns[k, group * LANES + s]
                row = spot // tiles
                at = pl.ds(pl.multiple_of((spot % tiles) * LANES, LANES), LANES)
                for step in range(STEPS):
                    value = pltpu.roll(heights[step, HALO + row, :, at], turn, 1)
                    fresh_held[step * points + k] = jnp.where(here, value, held[step * points + k])
            return tuple(fresh_held)

        zero = jnp.zeros((8, LANES), jnp.float32)
        held = lax.fori_loop(0, LANES, pick, (zero,) * (STEPS * points))
        for step in range(STEPS):
            total = None
            for k in range(points):
                term = obs_weight[pl.ds(k, 1), pl.ds(group * LANES, LANES)] * held[step * points + k]
                total = term if total is None else total + term
            out[step, group] = total


def run_model(spots, turns, low_c, centre, high_c, obs_weight, own, low, high):
    fields, rows, members, columns = own.shape
    tall = rows + 2 * HALO
    smem = pl.BlockSpec(memory_space=pltpu.SMEM)
    vmem = pl.BlockSpec(memory_space=pltpu.VMEM)
    raw = pl.BlockSpec(memory_space=pl.ANY)
    groups = obs_weight.shape[1] // LANES
    return pl.pallas_call(
        model_kernel,
        in_specs=[smem, smem, vmem, vmem, vmem, vmem, raw, raw, raw],
        out_specs=vmem,
        out_shape=jax.ShapeDtypeStruct((STEPS, groups, members, LANES), jnp.float32),
        scratch_shapes=[
            pltpu.VMEM((fields, tall, members, columns), jnp.float32),
            pltpu.VMEM((STEPS, tall, members, columns), jnp.float32),
            pltpu.VMEM((2, tall, members, columns), jnp.float32),
            pltpu.SemaphoreType.DMA((3,)),
        ],
        compiler_params=pltpu.CompilerParams(vmem_limit_bytes=56 << 20),
        name="model",
    )(spots, turns, low_c, centre, high_c, obs_weight, own, low, high)


def statistics_kernel(every, own, value, var, anom, packed):
    sources, steps, groups, members, _ = every.shape
    total = sources * members
    gram = jnp.zeros((total, total), jnp.float32)
    pull = jnp.zeros((total, 1), jnp.float32)
    for step in range(steps):
        for group in range(groups):
            at = pl.ds(group * LANES, LANES)
            y = every[:, step, group].reshape(total, LANES)
            mean = jnp.sum(y, axis=0, keepdims=True) * (1.0 / total)
            anom[:, step, at] = (own[step, group] - mean) / perturb
            flat = (y - mean) / perturb
            weighted = flat * (1.0 / var[pl.ds(step, 1), at])
            gram = gram + lax.dot_general(
                weighted,
                flat,
                (((1,), (1,)), ((), ())),
                precision=lax.Precision.HIGHEST,
                preferred_element_type=jnp.float32,
            )
            innov = value[pl.ds(step, 1), at] - mean
            pull = pull + jnp.sum(weighted * innov, axis=1, keepdims=True)
    packed[:, pl.ds(0, total)] = gram
    packed[:, pl.ds(total, LANES - total)] = jnp.broadcast_to(pull, (total, LANES - total))


def statistics(every, own, value, var):
    sources, steps, groups, members, _ = every.shape
    return pl.pallas_call(
        statistics_kernel,
        out_shape=[
            jax.ShapeDtypeStruct((members, steps, groups * LANES), jnp.float32),
            jax.ShapeDtypeStruct((sources * members, LANES), jnp.float32),
        ],
        name="statistics",
    )(every, own, value, var)


def body(
    anomalies,
    mean_state,
    weights,
    station_row,
    station_col,
    stencil_row,
    stencil_col,
    obs_weight,
    obs_value,
    obs_var,
):
    members, fields, rows, columns = anomalies.shape
    total = weights.shape[0]
    place = lax.axis_index("mem")
    chunks = lax.axis_size("mem")
    width = columns // chunks

    col = (station_col[None, :] + stencil_col) % columns
    spots = (station_row[None, :] + stencil_row) * (columns // LANES) + col // LANES
    slot = jnp.arange(col.shape[1], dtype=jnp.int32)[None, :]
    turns = (slot - col) % LANES

    own, top, bottom, partial_sum = prepare(place.reshape(1), weights, anomalies)
    low = lax.ppermute(bottom, "sp", ring("sp", 1))
    high = lax.ppermute(top, "sp", ring("sp", -1))

    pieces = lax.all_to_all(partial_sum, "mem", 0, 0, tiled=True)
    mean_piece = lax.dynamic_slice_in_dim(mean_state, place * width, width, 2)
    centre_piece = mean_piece + jnp.sum(pieces, axis=0)
    centre = lax.all_to_all(
        jnp.broadcast_to(centre_piece[None], (chunks, *centre_piece.shape)), "mem", 0, 0, tiled=True
    )
    edge = 8
    low_c = lax.ppermute(centre[:, :, rows - edge :], "sp", ring("sp", 1))
    high_c = lax.ppermute(centre[:, :, :edge], "sp", ring("sp", -1))

    seen = run_model(spots, turns, low_c, centre, high_c, obs_weight, own, low, high)
    every = lax.all_to_all(jnp.broadcast_to(seen[None], (chunks, *seen.shape)), "mem", 0, 0, tiled=True)
    obs_anom, packed = statistics(every, seen, obs_value, obs_var)
    count = lax.axis_size("sp")
    hop = 1
    while hop < count:
        packed = packed + lax.ppermute(packed, "sp", [(i, i ^ hop) for i in range(count)])
        hop *= 2
    hessian = packed[:, :total] + (total - 1) * jnp.eye(total, dtype=jnp.float32)
    gradient = (total - 1) * weights - packed[:, total]
    return (obs_anom, gradient, hessian)


def solution(mesh):
    return jax.shard_map(
        body,
        mesh=mesh,
        in_specs=(
            P("mem", None, "sp", None),
            P(None, "sp", None),
            P(),
            P("sp"),
            P("sp"),
            P(None, "sp"),
            P(None, "sp"),
            P(None, "sp"),
            P(None, "sp"),
            P(None, "sp"),
        ),
        out_specs=(P("mem", None, "sp"), P(), P()),
        check_vma=False,
    )
```

```python
import jax
import jax.numpy as jnp
from jax import lax
from jax.experimental import pallas as pl
from jax.experimental.pallas import tpu as pltpu
from jax.sharding import PartitionSpec as P

STEPS = 4
HALO = 2 * STEPS - 1
EARLY = 3
LANES = 128
GROUP = 4
PAIR = 2
SPAN = 4
NEAR = 4
VMEM_MODEL = 38 << 20
ROWS = 2

time_step = 1.0
coriolis = 0.1
perturb = 0.1


def in_hbm(array):
    return pltpu.with_memory_space_constraint(array, pltpu.HBM)


def ring(axis, step):
    count = lax.axis_size(axis)
    return [(i, (i + step) % count) for i in range(count)]


def prepare_kernel(place, weights, anom, turned, top, top_more, bottom, bottom_more, partial):
    members, rows = anom.shape[0], anom.shape[2]
    chunks, width = partial.shape[0], partial.shape[3]
    first = place[0] * members
    scales = [weights[first + m] for m in range(members)]

    per = width // (SPAN * LANES)

    def columns(c, carry):
        swapped, totals = [], []
        for i in range(SPAN):
            block = anom[:, 0, :, pl.ds(pl.multiple_of((c * SPAN + i) * LANES, LANES), LANES)]
            swapped.append(jnp.swapaxes(block, 0, 1))
            total = scales[0] * block[0]
            for m in range(1, members):
                total = total + scales[m] * block[m]
            totals.append(total)
        inner = pl.multiple_of(lax.rem(c, per) * (SPAN * LANES), SPAN * LANES)
        for i in range(SPAN):
            turned[0, :, c * SPAN + i] = swapped[i]
            partial[lax.div(c, per), 0, :, pl.ds(inner + i * LANES, LANES)] = totals[i]
        return carry

    lax.fori_loop(0, chunks * per, columns, 0)

    @pl.when(pl.program_id(1) == 0)
    def _():
        top[0] = turned[0, :EARLY]
        top_more[0] = turned[0, EARLY:HALO]

    @pl.when(pl.program_id(1) == 1)
    def _():
        bottom[0] = turned[0, rows - HALO : rows - HALO + EARLY]
        bottom_more[0] = turned[0, rows - HALO + EARLY :]


def prepare(place, weights, anomalies):
    members, fields, rows, columns = anomalies.shape
    half = rows // 2
    chunks = NEAR
    width = columns // chunks
    smem = pl.BlockSpec(memory_space=pltpu.SMEM)
    tiles = columns // LANES
    parts = (EARLY, HALO - EARLY) * 2
    return pl.pallas_call(
        prepare_kernel,
        grid=(fields, 2),
        in_specs=[smem, smem, pl.BlockSpec((members, 1, half, columns), lambda f, r: (0, f, r, 0))],
        out_specs=[
            pl.BlockSpec((1, half, tiles, members, LANES), lambda f, r: (f, r, 0, 0, 0)),
            *(pl.BlockSpec((1, part, tiles, members, LANES), lambda f, r: (f, 0, 0, 0, 0)) for part in parts),
            pl.BlockSpec((chunks, 1, half, width), lambda f, r: (0, f, r, 0)),
        ],
        out_shape=[
            pltpu.HBM((fields, rows, tiles, members, LANES), jnp.float32),
            *(pltpu.HBM((fields, part, tiles, members, LANES), jnp.float32) for part in parts),
            jax.ShapeDtypeStruct((chunks, fields, rows, width), jnp.float32),
        ],
        compiler_params=pltpu.CompilerParams(vmem_limit_bytes=40 << 20),
        name="prepare",
    )(place, weights, anomalies)


def model_kernel(
    spots, turns, low_c, centre, high_c, obs_weight, own, low, low_more, high, high_more, out, state, heights, spare, sems
):
    rows, tiles = own.shape[1], own.shape[2]
    tall = rows + 2 * HALO
    copies = []
    row = 0
    for source in (low, low_more, own, high, high_more):
        part = source.shape[1]
        for f in range(3):
            target = state.at[f, pl.ds(row, part)]
            copies.append(pltpu.make_async_copy(source.at[f], target, sems.at[len(copies)]))
        row += part
    for copy in copies:
        copy.start()
    for copy in copies:
        copy.wait()

    lane = lax.broadcasted_iota(jnp.int32, (8, LANES), 1)
    is_first = lane == 0
    is_last = lane == LANES - 1
    chunk_width = centre.shape[3]
    per = chunk_width // LANES

    edge = low_c.shape[2]

    def begin(i, carry):
        f = lax.div(i, tiles // PAIR)
        first = lax.rem(i, tiles // PAIR) * PAIR
        chunk = lax.div(first, per)
        inner = pl.multiple_of(lax.rem(first, per) * LANES, PAIR * LANES)
        for base, skip, at, count in (
            (low_c, edge - HALO, 0, HALO),
            (centre, 0, HALO, rows),
            (high_c, 0, HALO + rows, HALO),
        ):
            ready = []
            for r in range(count):
                for t in range(PAIR):
                    middle = base[chunk, f, pl.ds(skip + r, 1), pl.ds(inner + t * LANES, LANES)]
                    ready.append((r, t, middle + perturb * state[f, at + r, first + t]))
            for r, t, value in ready:
                state[f, at + r, first + t] = value
        return carry

    lax.fori_loop(0, 3 * tiles // PAIR, begin, 0)

    def memo(fetch):
        kept = {}

        def get(t):
            if isinstance(t, int):
                t %= tiles
            if t not in kept:
                kept[t] = fetch(t)
            return kept[t]

        return get

    def slope(piece):
        left = memo(lambda t: pltpu.roll(piece(t), LANES - 1, 1))
        right = memo(lambda t: pltpu.roll(piece(t), 1, 1))
        return lambda t: jnp.where(is_last, left(t + 1), left(t)) - jnp.where(is_first, right(t - 1), right(t))

    def rows_of(field, r):
        return memo(lambda key: field(r + key[0], key[1] % tiles))

    def in_row(get, i):
        return memo(lambda t: get((i, t)))

    def sweep(make, puts, r):
        for start in range(0, tiles, GROUP):
            span = range(start, start + GROUP)
            ready = [[make[i](t) for t in span] for i in range(len(make))]
            for i, values in enumerate(ready):
                for t, value in zip(span, values):
                    for put, part in zip(puts, value):
                        put(r + i, t, part)

    def height_rows(h, u, v, hn, r):
        gh, gu = rows_of(h, r), rows_of(u, r)
        flow = memo(lambda key: (1.0 + gh(key)) * gu(key))

        def row(i):
            across = slope(memo(lambda t: (1.0 + gh((i, t))) * v(r + i, t)))

            def value(t):
                along = flow((i + 1, t)) - flow((i - 1, t))
                return (gh((i, t)) - (0.5 * time_step) * (along + across(t)),)

            return value

        sweep([row(i) for i in range(ROWS)], (hn,), r)

    def momentum_rows(h, u, v, un, vn, r):
        gh, gu, gv = rows_of(h, r), rows_of(u, r), rows_of(v, r)

        def row(i):
            slope_h, slope_u, slope_v = slope(in_row(gh, i)), slope(in_row(gu, i)), slope(in_row(gv, i))

            def value(t):
                cu, cv = gu((i, t)), gv((i, t))
                du = (gh((i + 1, t)) - gh((i - 1, t))) + cu * (gu((i + 1, t)) - gu((i - 1, t))) + cv * slope_u(t)
                dv = slope_h(t) + cu * (gv((i + 1, t)) - gv((i - 1, t))) + cv * slope_v(t)
                return (
                    cu + (time_step * coriolis) * cv - (0.5 * time_step) * du,
                    cv - (time_step * coriolis) * cu - (0.5 * time_step) * dv,
                )

            return value

        sweep([row(i) for i in range(ROWS)], (un, vn), r)

    def reader(ref, *lead):
        return lambda r, t: ref[(*lead, r, t)]

    def writer(ref, *lead):
        def put(r, t, value):
            ref[(*lead, r, t)] = value

        return put

    h = (state, 0)
    pairs = [((state, 1), (state, 2)), ((spare, 0), (spare, 1))]
    for step in range(STEPS):
        (u, v), (un, vn) = pairs[step % 2], pairs[1 - step % 2]
        low_row = 2 * step + 1
        fresh = (heights, step)

        def height_body(i, carry):
            height_rows(reader(*h), reader(*u), reader(*v), writer(*fresh), low_row + ROWS * i)
            return carry

        lax.fori_loop(0, (tall - 2 * low_row) // ROWS, height_body, 0)
        if step + 1 < STEPS:

            def momentum_body(i, carry):
                momentum_rows(reader(*fresh), reader(*u), reader(*v), writer(*un), writer(*vn), low_row + 1 + ROWS * i)
                return carry

            lax.fori_loop(0, (tall - 2 * low_row - 2) // ROWS, momentum_body, 0)
        h = fresh

    points = obs_weight.shape[0]
    stations = obs_weight.shape[1]
    for group in range(stations // LANES):

        def pick(s, held):
            here = lane == s
            fresh_held = list(held)
            for k in range(points):
                spot = spots[k, group * LANES + s]
                turn = turns[k, group * LANES + s]
                for step in range(STEPS):
                    value = pltpu.roll(heights[step, HALO + lax.shift_right_logical(spot, tiles.bit_length() - 1), spot & (tiles - 1)], turn, 1)
                    fresh_held[step * points + k] = jnp.where(here, value, held[step * points + k])
            return tuple(fresh_held)

        zero = jnp.zeros((8, LANES), jnp.float32)
        held = lax.fori_loop(0, LANES, pick, (zero,) * (STEPS * points), unroll=16)
        for step in range(STEPS):
            total = None
            for k in range(points):
                term = obs_weight[pl.ds(k, 1), pl.ds(group * LANES, LANES)] * held[step * points + k]
                total = term if total is None else total + term
            out[step, group] = total


def run_model(spots, turns, low_c, centre, high_c, obs_weight, own, *halos):
    fields, rows, tiles, members, _ = own.shape
    tall = rows + 2 * HALO
    smem = pl.BlockSpec(memory_space=pltpu.SMEM)
    vmem = pl.BlockSpec(memory_space=pltpu.VMEM)
    groups = obs_weight.shape[1] // LANES
    return pl.pallas_call(
        model_kernel,
        in_specs=[smem, smem] + [vmem] * 4 + [pl.BlockSpec(memory_space=pltpu.HBM)] * 5,
        out_specs=vmem,
        out_shape=jax.ShapeDtypeStruct((STEPS, groups, members, LANES), jnp.float32),
        scratch_shapes=[
            pltpu.VMEM((fields, tall, tiles, members, LANES), jnp.float32),
            pltpu.VMEM((STEPS, tall, tiles, members, LANES), jnp.float32),
            pltpu.VMEM((2, tall, tiles, members, LANES), jnp.float32),
            pltpu.SemaphoreType.DMA((15,)),
        ],
        compiler_params=pltpu.CompilerParams(vmem_limit_bytes=VMEM_MODEL),
        name="model",
    )(spots, turns, low_c, centre, high_c, obs_weight, own, *halos)


def statistics_kernel(every, own, value, var, anom, packed):
    sources, steps, groups, members, _ = every.shape
    total = sources * members
    gram = jnp.zeros((total, total), jnp.float32)
    pull = jnp.zeros((total, 1), jnp.float32)
    for step in range(steps):
        for group in range(groups):
            at = pl.ds(group * LANES, LANES)
            y = every[:, step, group].reshape(total, LANES)
            mean = jnp.sum(y, axis=0, keepdims=True) * (1.0 / total)
            anom[:, step, at] = (own[step, group] - mean) / perturb
            flat = (y - mean) / perturb
            weighted = flat * (1.0 / var[pl.ds(step, 1), at])
            gram = gram + lax.dot_general(
                weighted,
                flat,
                (((1,), (1,)), ((), ())),
                precision=lax.Precision.HIGHEST,
                preferred_element_type=jnp.float32,
            )
            innov = value[pl.ds(step, 1), at] - mean
            pull = pull + jnp.sum(weighted * innov, axis=1, keepdims=True)
    packed[:, pl.ds(0, total)] = gram
    packed[:, pl.ds(total, LANES - total)] = jnp.broadcast_to(pull, (total, LANES - total))


def statistics(every, own, value, var):
    sources, steps, groups, members, _ = every.shape
    return pl.pallas_call(
        statistics_kernel,
        out_shape=[
            jax.ShapeDtypeStruct((members, steps, groups * LANES), jnp.float32),
            jax.ShapeDtypeStruct((sources * members, LANES), jnp.float32),
        ],
        name="statistics",
    )(every, own, value, var)


def body(
    anomalies,
    mean_state,
    weights,
    station_row,
    station_col,
    stencil_row,
    stencil_col,
    obs_weight,
    obs_value,
    obs_var,
):
    members, fields, rows, columns = anomalies.shape
    total = weights.shape[0]
    place = lax.axis_index("mem")
    count = lax.axis_size("mem")
    near = [[start + i for i in range(NEAR)] for start in range(0, count, NEAR)]
    width = columns // NEAR

    col = (station_col[None, :] + stencil_col) % columns
    spots = (station_row[None, :] + stencil_row) * (columns // LANES) + col // LANES
    slot = jnp.arange(col.shape[1], dtype=jnp.int32)[None, :]
    turns = (slot - col) % LANES

    own, top, top_more, bottom, bottom_more, partial_sum = prepare(place.reshape(1), weights, in_hbm(anomalies))
    low = lax.ppermute(bottom, "sp", ring("sp", 1))
    high = lax.ppermute(top, "sp", ring("sp", -1))

    pieces = lax.all_to_all(partial_sum, "mem", 0, 0, axis_index_groups=near, tiled=True)
    piece = jnp.sum(pieces, axis=0)
    piece, low, high = lax.optimization_barrier((piece, low, high))
    hop = NEAR
    while hop < count:
        piece = piece + lax.ppermute(piece, "mem", [(i, i ^ hop) for i in range(count)])
        hop *= 2
    piece, top_more, bottom_more = lax.optimization_barrier((piece, top_more, bottom_more))
    low_more = lax.ppermute(bottom_more, "sp", ring("sp", 1))
    high_more = lax.ppermute(top_more, "sp", ring("sp", -1))
    piece = piece + lax.dynamic_slice_in_dim(mean_state, lax.rem(place, NEAR) * width, width, 2)
    centre = lax.all_to_all(
        jnp.broadcast_to(piece[None], (NEAR, *piece.shape)), "mem", 0, 0, axis_index_groups=near, tiled=True
    )
    edge = 8
    low_c = lax.ppermute(centre[:, :, rows - edge :], "sp", ring("sp", 1))
    high_c = lax.ppermute(centre[:, :, :edge], "sp", ring("sp", -1))

    seen = run_model(spots, turns, low_c, centre, high_c, obs_weight, *map(in_hbm, (own, low, low_more, high, high_more)))
    every = lax.all_to_all(jnp.broadcast_to(seen[None], (count, *seen.shape)), "mem", 0, 0, tiled=True)
    obs_anom, packed = statistics(every, seen, obs_value, obs_var)
    count = lax.axis_size("sp")
    hop = 1
    while hop < count:
        packed = packed + lax.ppermute(packed, "sp", [(i, i ^ hop) for i in range(count)])
        hop *= 2
    hessian = packed[:, :total] + (total - 1) * jnp.eye(total, dtype=jnp.float32)
    gradient = (total - 1) * weights - packed[:, total]
    return (obs_anom, gradient, hessian)


def solution(mesh):
    return jax.shard_map(
        body,
        mesh=mesh,
        in_specs=(
            P("mem", None, "sp", None),
            P(None, "sp", None),
            P(),
            P("sp"),
            P("sp"),
            P(None, "sp"),
            P(None, "sp"),
            P(None, "sp"),
            P(None, "sp"),
            P(None, "sp"),
        ),
        out_specs=(P("mem", None, "sp"), P(), P()),
        check_vma=False,
    )
```

```python
import functools

import jax
import jax.numpy as jnp
from jax import lax
from jax.experimental import pallas as pl
from jax.experimental.pallas import tpu as pltpu
from jax.sharding import PartitionSpec as P

STEPS = 4
HALO = 2 * STEPS - 1
EARLY = 3
LANES = 128
GROUP = 4
PAIR = 4
SPAN = 4
NEAR = 4
VMEM_MODEL = 38 << 20
ROWS = 2

time_step = 1.0
coriolis = 0.1
perturb = 0.1


def in_hbm(array):
    return pltpu.with_memory_space_constraint(array, pltpu.HBM)


def ring(axis, step):
    count = lax.axis_size(axis)
    return [(i, (i + step) % count) for i in range(count)]


def prepare_kernel(place, weights, anom, *outs):
    *parts, partial = outs
    members, half = anom.shape[0], anom.shape[2]
    chunks, width = partial.shape[0], partial.shape[3]
    first = place[0] * members
    scales = [weights[first + m] for m in range(members)]
    per = width // (SPAN * LANES)
    homes = [(part, r) for part in parts for r in range(part.shape[1])]

    def turn(homes):
        def columns(c, carry):
            swapped, totals = [], []
            for i in range(SPAN):
                block = anom[:, 0, :, pl.ds(pl.multiple_of((c * SPAN + i) * LANES, LANES), LANES)]
                swapped.append(jnp.swapaxes(block, 0, 1))
                total = scales[0] * block[0]
                for m in range(1, members):
                    total = total + scales[m] * block[m]
                totals.append(total)
            inner = pl.multiple_of(lax.rem(c, per) * (SPAN * LANES), SPAN * LANES)
            for i in range(SPAN):
                for r, (part, home) in enumerate(homes):
                    part[0, home, c * SPAN + i] = swapped[i][r]
                partial[lax.div(c, per), 0, :, pl.ds(inner + i * LANES, LANES)] = totals[i]
            return carry

        lax.fori_loop(0, chunks * per, columns, 0)

    for step in range(2):

        @pl.when(pl.program_id(1) == step)
        def _():
            turn(homes[step * half : (step + 1) * half])


def prepare(place, weights, anomalies):
    members, fields, rows, columns = anomalies.shape
    half = rows // 2
    chunks = NEAR
    width = columns // chunks
    smem = pl.BlockSpec(memory_space=pltpu.SMEM)
    tiles = columns // LANES
    late = HALO - EARLY
    parts = (EARLY, late, rows - 2 * HALO, EARLY, late)
    return pl.pallas_call(
        prepare_kernel,
        grid=(fields, 2),
        in_specs=[smem, smem, pl.BlockSpec((members, 1, half, columns), lambda f, r: (0, f, r, 0))],
        out_specs=[
            *(pl.BlockSpec((1, part, tiles, members, LANES), lambda f, r: (f, 0, 0, 0, 0)) for part in parts),
            pl.BlockSpec((chunks, 1, half, width), lambda f, r: (0, f, r, 0)),
        ],
        out_shape=[
            *(pltpu.HBM((fields, part, tiles, members, LANES), jnp.float32) for part in parts),
            jax.ShapeDtypeStruct((chunks, fields, rows, width), jnp.float32),
        ],
        compiler_params=pltpu.CompilerParams(vmem_limit_bytes=40 << 20),
        name="prepare",
    )(place, weights, anomalies)


def model_kernel(
    spots, turns, low_c, centre, high_c, obs_weight, *refs
):
    *sources, out, state, heights, spare, sems = refs
    tall, tiles = state.shape[1], state.shape[2]
    rows = tall - 2 * HALO
    copies = []
    for f in range(3):
        row = 0
        for i, source in enumerate(sources):
            part = source.shape[1]
            copies.append(pltpu.make_async_copy(source.at[f], state.at[f, pl.ds(row, part)], sems.at[f, i]))
            row += part
    for copy in copies:
        copy.start()

    lane = lax.broadcasted_iota(jnp.int32, (8, LANES), 1)
    is_first = lane == 0
    is_last = lane == LANES - 1
    chunk_width = centre.shape[3]
    per = chunk_width // LANES

    edge = low_c.shape[2]

    def begin(f, i, carry):
        first = i * PAIR
        chunk = lax.div(first, per)
        inner = pl.multiple_of(lax.rem(first, per) * LANES, PAIR * LANES)
        for base, skip, at, count in (
            (low_c, edge - HALO, 0, HALO),
            (centre, 0, HALO, rows),
            (high_c, 0, HALO + rows, HALO),
        ):
            ready = []
            for r in range(count):
                for t in range(PAIR):
                    middle = base[chunk, f, pl.ds(skip + r, 1), pl.ds(inner + t * LANES, LANES)]
                    ready.append((r, t, middle + perturb * state[f, at + r, first + t]))
            for r, t, value in ready:
                state[f, at + r, first + t] = value
        return carry

    for f in range(3):
        for copy in copies[f * len(sources) : (f + 1) * len(sources)]:
            copy.wait()
        lax.fori_loop(0, tiles // PAIR, functools.partial(begin, f), 0)

    def memo(fetch):
        kept = {}

        def get(t):
            if isinstance(t, int):
                t %= tiles
            if t not in kept:
                kept[t] = fetch(t)
            return kept[t]

        return get

    def slope(piece):
        left = memo(lambda t: pltpu.roll(piece(t), LANES - 1, 1))
        right = memo(lambda t: pltpu.roll(piece(t), 1, 1))
        return lambda t: jnp.where(is_last, left(t + 1), left(t)) - jnp.where(is_first, right(t - 1), right(t))

    def rows_of(field, r):
        return memo(lambda key: field(r + key[0], key[1] % tiles))

    def in_row(get, i):
        return memo(lambda t: get((i, t)))

    def sweep(make, puts, r):
        for start in range(0, tiles, GROUP):
            span = range(start, start + GROUP)
            ready = [[make[i](t) for t in span] for i in range(len(make))]
            for i, values in enumerate(ready):
                for t, value in zip(span, values):
                    for put, part in zip(puts, value):
                        put(r + i, t, part)

    def height_rows(h, u, v, hn, r):
        gh, gu = rows_of(h, r), rows_of(u, r)
        flow = memo(lambda key: (1.0 + gh(key)) * gu(key))

        def row(i):
            across = slope(memo(lambda t: (1.0 + gh((i, t))) * v(r + i, t)))

            def value(t):
                along = flow((i + 1, t)) - flow((i - 1, t))
                return (gh((i, t)) - (0.5 * time_step) * (along + across(t)),)

            return value

        sweep([row(i) for i in range(2 * ROWS)], (hn,), r)

    def momentum_rows(h, u, v, un, vn, r):
        gh, gu, gv = rows_of(h, r), rows_of(u, r), rows_of(v, r)

        def row(i):
            slope_h, slope_u, slope_v = slope(in_row(gh, i)), slope(in_row(gu, i)), slope(in_row(gv, i))

            def value(t):
                cu, cv = gu((i, t)), gv((i, t))
                du = (gh((i + 1, t)) - gh((i - 1, t))) + cu * (gu((i + 1, t)) - gu((i - 1, t))) + cv * slope_u(t)
                dv = slope_h(t) + cu * (gv((i + 1, t)) - gv((i - 1, t))) + cv * slope_v(t)
                return (
                    cu + (time_step * coriolis) * cv - (0.5 * time_step) * du,
                    cv - (time_step * coriolis) * cu - (0.5 * time_step) * dv,
                )

            return value

        sweep([row(i) for i in range(ROWS)], (un, vn), r)

    def reader(ref, *lead):
        return lambda r, t: ref[(*lead, r, t)]

    def writer(ref, *lead):
        def put(r, t, value):
            ref[(*lead, r, t)] = value

        return put

    h = (state, 0)
    pairs = [((state, 1), (state, 2)), ((spare, 0), (spare, 1))]
    for step in range(STEPS):
        (u, v), (un, vn) = pairs[step % 2], pairs[1 - step % 2]
        low_row = 2 * step + 1
        fresh = (heights, step)

        def height_body(i, carry):
            height_rows(reader(*h), reader(*u), reader(*v), writer(*fresh), low_row + 2 * ROWS * i)
            return carry

        lax.fori_loop(0, (tall - 2 * low_row) // (2 * ROWS), height_body, 0)
        if step + 1 < STEPS:

            def momentum_body(i, carry):
                momentum_rows(reader(*fresh), reader(*u), reader(*v), writer(*un), writer(*vn), low_row + 1 + ROWS * i)
                return carry

            lax.fori_loop(0, (tall - 2 * low_row - 2) // ROWS, momentum_body, 0)
        h = fresh

    points = obs_weight.shape[0]
    stations = obs_weight.shape[1]
    for group in range(stations // LANES):

        def pick(s, held):
            here = lane == s
            fresh_held = list(held)
            for k in range(points):
                spot = spots[k, group * LANES + s]
                turn = turns[k, group * LANES + s]
                for step in range(STEPS):
                    value = pltpu.roll(heights[step, HALO + lax.shift_right_logical(spot, tiles.bit_length() - 1), spot & (tiles - 1)], turn, 1)
                    fresh_held[step * points + k] = jnp.where(here, value, held[step * points + k])
            return tuple(fresh_held)

        zero = jnp.zeros((8, LANES), jnp.float32)
        held = lax.fori_loop(0, LANES, pick, (zero,) * (STEPS * points), unroll=16)
        for step in range(STEPS):
            total = None
            for k in range(points):
                term = obs_weight[pl.ds(k, 1), pl.ds(group * LANES, LANES)] * held[step * points + k]
                total = term if total is None else total + term
            out[step, group] = total


def run_model(spots, turns, low_c, centre, high_c, obs_weight, *parts):
    fields, _, tiles, members, _ = parts[0].shape
    tall = sum(part.shape[1] for part in parts)
    smem = pl.BlockSpec(memory_space=pltpu.SMEM)
    vmem = pl.BlockSpec(memory_space=pltpu.VMEM)
    groups = obs_weight.shape[1] // LANES
    return pl.pallas_call(
        model_kernel,
        in_specs=[smem, smem] + [vmem] * 4 + [pl.BlockSpec(memory_space=pl.ANY)] * len(parts),
        out_specs=vmem,
        out_shape=jax.ShapeDtypeStruct((STEPS, groups, members, LANES), jnp.float32),
        scratch_shapes=[
            pltpu.VMEM((fields, tall, tiles, members, LANES), jnp.float32),
            pltpu.VMEM((STEPS, tall, tiles, members, LANES), jnp.float32),
            pltpu.VMEM((2, tall, tiles, members, LANES), jnp.float32),
            pltpu.SemaphoreType.DMA((fields, len(parts))),
        ],
        compiler_params=pltpu.CompilerParams(vmem_limit_bytes=VMEM_MODEL),
        name="model",
    )(spots, turns, low_c, centre, high_c, obs_weight, *parts)


def statistics_kernel(every, own, value, var, anom, packed):
    sources, steps, groups, members, _ = every.shape
    total = sources * members
    gram = jnp.zeros((total, total), jnp.float32)
    pull = jnp.zeros((total, 1), jnp.float32)
    for step in range(steps):
        for group in range(groups):
            at = pl.ds(group * LANES, LANES)
            y = every[:, step, group].reshape(total, LANES)
            mean = jnp.sum(y, axis=0, keepdims=True) * (1.0 / total)
            anom[:, step, at] = (own[step, group] - mean) / perturb
            flat = (y - mean) / perturb
            weighted = flat * (1.0 / var[pl.ds(step, 1), at])
            gram = gram + lax.dot_general(
                weighted,
                flat,
                (((1,), (1,)), ((), ())),
                precision=lax.Precision.HIGHEST,
                preferred_element_type=jnp.float32,
            )
            innov = value[pl.ds(step, 1), at] - mean
            pull = pull + jnp.sum(weighted * innov, axis=1, keepdims=True)
    packed[:, pl.ds(0, total)] = gram
    packed[:, pl.ds(total, LANES - total)] = jnp.broadcast_to(pull, (total, LANES - total))


def statistics(every, own, value, var):
    sources, steps, groups, members, _ = every.shape
    return pl.pallas_call(
        statistics_kernel,
        out_shape=[
            jax.ShapeDtypeStruct((members, steps, groups * LANES), jnp.float32),
            jax.ShapeDtypeStruct((sources * members, LANES), jnp.float32),
        ],
        name="statistics",
    )(every, own, value, var)


def body(
    anomalies,
    mean_state,
    weights,
    station_row,
    station_col,
    stencil_row,
    stencil_col,
    obs_weight,
    obs_value,
    obs_var,
):
    members, fields, rows, columns = anomalies.shape
    total = weights.shape[0]
    place = lax.axis_index("mem")
    count = lax.axis_size("mem")
    near = [[start + i for i in range(NEAR)] for start in range(0, count, NEAR)]
    width = columns // NEAR

    col = (station_col[None, :] + stencil_col) % columns
    spots = (station_row[None, :] + stencil_row) * (columns // LANES) + col // LANES
    slot = jnp.arange(col.shape[1], dtype=jnp.int32)[None, :]
    turns = (slot - col) % LANES

    top, top_more, middle, bottom, bottom_more, partial_sum = prepare(place.reshape(1), weights, in_hbm(anomalies))
    own = [in_hbm(part) for part in (top, top_more, middle, bottom, bottom_more)]
    low = lax.ppermute(bottom, "sp", ring("sp", 1))
    high = lax.ppermute(top, "sp", ring("sp", -1))

    pieces = lax.all_to_all(partial_sum, "mem", 0, 0, axis_index_groups=near, tiled=True)
    piece = jnp.sum(pieces, axis=0)
    piece, low, high = lax.optimization_barrier((piece, low, high))
    hop = NEAR
    while hop < count:
        piece = piece + lax.ppermute(piece, "mem", [(i, i ^ hop) for i in range(count)])
        hop *= 2
    piece, top_more, bottom_more = lax.optimization_barrier((piece, top_more, bottom_more))
    low_more = lax.ppermute(bottom_more, "sp", ring("sp", 1))
    high_more = lax.ppermute(top_more, "sp", ring("sp", -1))
    piece = piece + lax.dynamic_slice_in_dim(mean_state, lax.rem(place, NEAR) * width, width, 2)
    centre = lax.all_to_all(
        jnp.broadcast_to(piece[None], (NEAR, *piece.shape)), "mem", 0, 0, axis_index_groups=near, tiled=True
    )
    edge = 8
    low_c = lax.ppermute(centre[:, :, rows - edge :], "sp", ring("sp", 1))
    high_c = lax.ppermute(centre[:, :, :edge], "sp", ring("sp", -1))

    seen = run_model(spots, turns, low_c, centre, high_c, obs_weight, in_hbm(low), low_more, *own, in_hbm(high), high_more)
    every = lax.all_to_all(jnp.broadcast_to(seen[None], (count, *seen.shape)), "mem", 0, 0, tiled=True)
    obs_anom, packed = statistics(every, seen, obs_value, obs_var)
    count = lax.axis_size("sp")
    hop = 1
    while hop < count:
        packed = packed + lax.ppermute(packed, "sp", [(i, i ^ hop) for i in range(count)])
        hop *= 2
    hessian = packed[:, :total] + (total - 1) * jnp.eye(total, dtype=jnp.float32)
    gradient = (total - 1) * weights - packed[:, total]
    return (obs_anom, gradient, hessian)


def solution(mesh):
    return jax.shard_map(
        body,
        mesh=mesh,
        in_specs=(
            P("mem", None, "sp", None),
            P(None, "sp", None),
            P(),
            P("sp"),
            P("sp"),
            P(None, "sp"),
            P(None, "sp"),
            P(None, "sp"),
            P(None, "sp"),
            P(None, "sp"),
        ),
        out_specs=(P("mem", None, "sp"), P(), P()),
        check_vma=False,
    )
```

```python
import functools

import jax
import jax.numpy as jnp
from jax import lax
from jax.experimental import pallas as pl
from jax.experimental.pallas import tpu as pltpu
from jax.sharding import PartitionSpec as P

STEPS = 4
HALO = 2 * STEPS - 1
EARLY = 3
LANES = 128
GROUP = 4
PAIR = 4
SPAN = 4
NEAR = 4
VMEM_MODEL = 38 << 20
ROWS = 2

time_step = 1.0
coriolis = 0.1
perturb = 0.1


def in_hbm(array):
    return pltpu.with_memory_space_constraint(array, pltpu.HBM)


def ring(axis, step):
    count = lax.axis_size(axis)
    return [(i, (i + step) % count) for i in range(count)]


def prepare_kernel(place, weights, anom, *outs):
    *parts, partial = outs
    members, half = anom.shape[0], anom.shape[2]
    chunks, width = partial.shape[0], partial.shape[3]
    first = place[0] * members
    scales = [weights[first + m] for m in range(members)]
    per = width // (SPAN * LANES)
    homes = [(part, r) for part in parts for r in range(part.shape[1])]

    def turn(homes):
        def columns(c, carry):
            swapped, totals = [], []
            for i in range(SPAN):
                block = anom[:, 0, :, pl.ds(pl.multiple_of((c * SPAN + i) * LANES, LANES), LANES)]
                swapped.append(jnp.swapaxes(block, 0, 1))
                total = scales[0] * block[0]
                for m in range(1, members):
                    total = total + scales[m] * block[m]
                totals.append(total)
            inner = pl.multiple_of(lax.rem(c, per) * (SPAN * LANES), SPAN * LANES)
            for i in range(SPAN):
                for r, (part, home) in enumerate(homes):
                    part[0, home, c * SPAN + i] = swapped[i][r]
                partial[lax.div(c, per), 0, :, pl.ds(inner + i * LANES, LANES)] = totals[i]
            return carry

        lax.fori_loop(0, chunks * per, columns, 0)

    for step in range(2):

        @pl.when(pl.program_id(1) == step)
        def _():
            turn(homes[step * half : (step + 1) * half])


def prepare(place, weights, anomalies):
    members, fields, rows, columns = anomalies.shape
    half = rows // 2
    chunks = NEAR
    width = columns // chunks
    smem = pl.BlockSpec(memory_space=pltpu.SMEM)
    tiles = columns // LANES
    late = HALO - EARLY
    parts = (EARLY, late, rows - 2 * HALO, EARLY, late)
    return pl.pallas_call(
        prepare_kernel,
        grid=(fields, 2),
        in_specs=[smem, smem, pl.BlockSpec((members, 1, half, columns), lambda f, r: (0, f, r, 0))],
        out_specs=[
            *(pl.BlockSpec((1, part, tiles, members, LANES), lambda f, r: (f, 0, 0, 0, 0)) for part in parts),
            pl.BlockSpec((chunks, 1, half, width), lambda f, r: (0, f, r, 0)),
        ],
        out_shape=[
            *(pltpu.HBM((fields, part, tiles, members, LANES), jnp.float32) for part in parts),
            jax.ShapeDtypeStruct((chunks, fields, rows, width), jnp.float32),
        ],
        compiler_params=pltpu.CompilerParams(vmem_limit_bytes=40 << 20),
        name="prepare",
    )(place, weights, anomalies)


def model_kernel(
    spots, lanes, low_c, centre, high_c, obs_weight, *refs
):
    *sources, out, state, heights, spare, sems = refs
    tall, tiles = state.shape[1], state.shape[2]
    rows = tall - 2 * HALO
    copies = []
    for f in range(3):
        row = 0
        for i, source in enumerate(sources):
            part = source.shape[1]
            copies.append(pltpu.make_async_copy(source.at[f], state.at[f, pl.ds(row, part)], sems.at[f, i]))
            row += part
    for copy in copies:
        copy.start()

    lane = lax.broadcasted_iota(jnp.int32, (8, LANES), 1)
    is_first = lane == 0
    is_last = lane == LANES - 1
    chunk_width = centre.shape[3]
    per = chunk_width // LANES

    edge = low_c.shape[2]

    def begin(f, i, carry):
        first = i * PAIR
        chunk = lax.div(first, per)
        inner = pl.multiple_of(lax.rem(first, per) * LANES, PAIR * LANES)
        for base, skip, at, count in (
            (low_c, edge - HALO, 0, HALO),
            (centre, 0, HALO, rows),
            (high_c, 0, HALO + rows, HALO),
        ):
            ready = []
            for r in range(count):
                for t in range(PAIR):
                    middle = base[chunk, f, pl.ds(skip + r, 1), pl.ds(inner + t * LANES, LANES)]
                    ready.append((r, t, middle + perturb * state[f, at + r, first + t]))
            for r, t, value in ready:
                state[f, at + r, first + t] = value
        return carry

    for f in range(3):
        for copy in copies[f * len(sources) : (f + 1) * len(sources)]:
            copy.wait()
        lax.fori_loop(0, tiles // PAIR, functools.partial(begin, f), 0)

    def memo(fetch):
        kept = {}

        def get(t):
            if isinstance(t, int):
                t %= tiles
            if t not in kept:
                kept[t] = fetch(t)
            return kept[t]

        return get

    def slope(piece):
        left = memo(lambda t: pltpu.roll(piece(t), LANES - 1, 1))
        right = memo(lambda t: pltpu.roll(piece(t), 1, 1))
        return lambda t: jnp.where(is_last, left(t + 1), left(t)) - jnp.where(is_first, right(t - 1), right(t))

    def rows_of(field, r):
        return memo(lambda key: field(r + key[0], key[1] % tiles))

    def in_row(get, i):
        return memo(lambda t: get((i, t)))

    def sweep(make, puts, r):
        for start in range(0, tiles, GROUP):
            span = range(start, start + GROUP)
            ready = [[make[i](t) for t in span] for i in range(len(make))]
            for i, values in enumerate(ready):
                for t, value in zip(span, values):
                    for put, part in zip(puts, value):
                        put(r + i, t, part)

    def height_rows(h, u, v, hn, r):
        gh, gu = rows_of(h, r), rows_of(u, r)
        flow = memo(lambda key: (1.0 + gh(key)) * gu(key))

        def row(i):
            across = slope(memo(lambda t: (1.0 + gh((i, t))) * v(r + i, t)))

            def value(t):
                along = flow((i + 1, t)) - flow((i - 1, t))
                return (gh((i, t)) - (0.5 * time_step) * (along + across(t)),)

            return value

        sweep([row(i) for i in range(2 * ROWS)], (hn,), r)

    def momentum_rows(h, u, v, un, vn, r):
        gh, gu, gv = rows_of(h, r), rows_of(u, r), rows_of(v, r)

        def row(i):
            slope_h, slope_u, slope_v = slope(in_row(gh, i)), slope(in_row(gu, i)), slope(in_row(gv, i))

            def value(t):
                cu, cv = gu((i, t)), gv((i, t))
                du = (gh((i + 1, t)) - gh((i - 1, t))) + cu * (gu((i + 1, t)) - gu((i - 1, t))) + cv * slope_u(t)
                dv = slope_h(t) + cu * (gv((i + 1, t)) - gv((i - 1, t))) + cv * slope_v(t)
                return (
                    cu + (time_step * coriolis) * cv - (0.5 * time_step) * du,
                    cv - (time_step * coriolis) * cu - (0.5 * time_step) * dv,
                )

            return value

        sweep([row(i) for i in range(ROWS)], (un, vn), r)

    def reader(ref, *lead):
        return lambda r, t: ref[(*lead, r, t)]

    def writer(ref, *lead):
        def put(r, t, value):
            ref[(*lead, r, t)] = value

        return put

    h = (state, 0)
    pairs = [((state, 1), (state, 2)), ((spare, 0), (spare, 1))]
    for step in range(STEPS):
        (u, v), (un, vn) = pairs[step % 2], pairs[1 - step % 2]
        low_row = 2 * step + 1
        fresh = (heights, step)

        def height_body(i, carry):
            height_rows(reader(*h), reader(*u), reader(*v), writer(*fresh), low_row + 2 * ROWS * i)
            return carry

        lax.fori_loop(0, (tall - 2 * low_row) // (2 * ROWS), height_body, 0)
        if step + 1 < STEPS:

            def momentum_body(i, carry):
                momentum_rows(reader(*fresh), reader(*u), reader(*v), writer(*un), writer(*vn), low_row + 1 + ROWS * i)
                return carry

            lax.fori_loop(0, (tall - 2 * low_row - 2) // ROWS, momentum_body, 0)
        h = fresh

    points, stations = spots.shape
    for group in range(stations // LANES):

        def pick(s, held):
            here = lane == s
            totals = [None] * STEPS
            for k in range(points):
                spot = spots[k, group * LANES + s]
                row, tile = HALO + lax.shift_right_logical(spot, tiles.bit_length() - 1), spot & (tiles - 1)
                factor = jnp.where(lane == lanes[k, group * LANES + s], obs_weight[k, group * LANES + s], 0.0)
                for step in range(STEPS):
                    value = factor * heights[step, row, tile]
                    totals[step] = value if totals[step] is None else totals[step] + value
            return tuple(
                jnp.where(here, jnp.sum(totals[step], axis=1, keepdims=True), held[step]) for step in range(STEPS)
            )

        zero = jnp.zeros((8, LANES), jnp.float32)
        held = lax.fori_loop(0, LANES, pick, (zero,) * STEPS, unroll=32)
        for step in range(STEPS):
            out[step, group] = held[step]


def run_model(spots, lanes, low_c, centre, high_c, obs_weight, *parts):
    fields, _, tiles, members, _ = parts[0].shape
    tall = sum(part.shape[1] for part in parts)
    smem = pl.BlockSpec(memory_space=pltpu.SMEM)
    vmem = pl.BlockSpec(memory_space=pltpu.VMEM)
    groups = obs_weight.shape[1] // LANES
    return pl.pallas_call(
        model_kernel,
        in_specs=[smem, smem, vmem, vmem, vmem, smem] + [pl.BlockSpec(memory_space=pl.ANY)] * len(parts),
        out_specs=vmem,
        out_shape=jax.ShapeDtypeStruct((STEPS, groups, members, LANES), jnp.float32),
        scratch_shapes=[
            pltpu.VMEM((fields, tall, tiles, members, LANES), jnp.float32),
            pltpu.VMEM((STEPS, tall, tiles, members, LANES), jnp.float32),
            pltpu.VMEM((2, tall, tiles, members, LANES), jnp.float32),
            pltpu.SemaphoreType.DMA((fields, len(parts))),
        ],
        compiler_params=pltpu.CompilerParams(vmem_limit_bytes=VMEM_MODEL),
        name="model",
    )(spots, lanes, low_c, centre, high_c, obs_weight, *parts)


def statistics_kernel(every, own, value, var, anom, packed):
    sources, steps, groups, members, _ = every.shape
    total = sources * members
    gram = jnp.zeros((total, total), jnp.float32)
    pull = jnp.zeros((1, total), jnp.float32)
    for step in range(steps):
        for group in range(groups):
            at = pl.ds(group * LANES, LANES)
            y = every[:, step, group].reshape(total, LANES)
            mean = jnp.sum(y, axis=0, keepdims=True) * (1.0 / total)
            anom[:, step, at] = (own[step, group] - mean) / perturb
            flat = (y - mean) / perturb
            weighted = flat * (1.0 / var[pl.ds(step, 1), at])
            innov = value[pl.ds(step, 1), at] - mean
            gram = gram + across(weighted, flat)
            pull = pull + across(innov, weighted)
    packed[pl.ds(0, total)] = gram
    packed[pl.ds(total, 8)] = jnp.broadcast_to(pull, (8, total))


def across(left, right):
    return lax.dot_general(
        left,
        right,
        (((1,), (1,)), ((), ())),
        precision=lax.Precision.HIGHEST,
        preferred_element_type=jnp.float32,
    )


def statistics(every, own, value, var):
    sources, steps, groups, members, _ = every.shape
    return pl.pallas_call(
        statistics_kernel,
        out_shape=[
            jax.ShapeDtypeStruct((members, steps, groups * LANES), jnp.float32),
            jax.ShapeDtypeStruct((sources * members + 8, sources * members), jnp.float32),
        ],
        name="statistics",
    )(every, own, value, var)


def body(
    anomalies,
    mean_state,
    weights,
    station_row,
    station_col,
    stencil_row,
    stencil_col,
    obs_weight,
    obs_value,
    obs_var,
):
    members, fields, rows, columns = anomalies.shape
    total = weights.shape[0]
    place = lax.axis_index("mem")
    count = lax.axis_size("mem")
    near = [[start + i for i in range(NEAR)] for start in range(0, count, NEAR)]
    width = columns // NEAR

    col = (station_col[None, :] + stencil_col) % columns
    spots = (station_row[None, :] + stencil_row) * (columns // LANES) + col // LANES
    lanes = col % LANES

    top, top_more, middle, bottom, bottom_more, partial_sum = prepare(place.reshape(1), in_hbm(weights), in_hbm(anomalies))
    own = [in_hbm(part) for part in (top, top_more, middle, bottom, bottom_more)]
    low = lax.ppermute(bottom, "sp", ring("sp", 1))
    high = lax.ppermute(top, "sp", ring("sp", -1))

    pieces = lax.all_to_all(partial_sum, "mem", 0, 0, axis_index_groups=near, tiled=True)
    piece = jnp.sum(pieces, axis=0)
    piece, low, high = lax.optimization_barrier((piece, low, high))
    hop = NEAR
    while hop < count:
        piece = piece + lax.ppermute(piece, "mem", [(i, i ^ hop) for i in range(count)])
        hop *= 2
    piece, top_more, bottom_more = lax.optimization_barrier((piece, top_more, bottom_more))
    low_more = lax.ppermute(bottom_more, "sp", ring("sp", 1))
    high_more = lax.ppermute(top_more, "sp", ring("sp", -1))
    piece = piece + lax.dynamic_slice_in_dim(mean_state, lax.rem(place, NEAR) * width, width, 2)
    centre = lax.all_to_all(
        jnp.broadcast_to(piece[None], (NEAR, *piece.shape)), "mem", 0, 0, axis_index_groups=near, tiled=True
    )
    edge = 8
    low_c = lax.ppermute(centre[:, :, rows - edge :], "sp", ring("sp", 1))
    high_c = lax.ppermute(centre[:, :, :edge], "sp", ring("sp", -1))

    seen = run_model(spots, lanes, low_c, centre, high_c, obs_weight, in_hbm(low), low_more, *own, in_hbm(high), high_more)
    every = lax.all_to_all(jnp.broadcast_to(seen[None], (count, *seen.shape)), "mem", 0, 0, tiled=True)
    obs_anom, packed = statistics(every, seen, obs_value, obs_var)
    count = lax.axis_size("sp")
    hop = 1
    while hop < count:
        packed = packed + lax.ppermute(packed, "sp", [(i, i ^ hop) for i in range(count)])
        hop *= 2
    hessian = packed[:total] + (total - 1) * jnp.eye(total, dtype=jnp.float32)
    gradient = (total - 1) * weights - packed[total]
    return (obs_anom, gradient, hessian)


def solution(mesh):
    return jax.shard_map(
        body,
        mesh=mesh,
        in_specs=(
            P("mem", None, "sp", None),
            P(None, "sp", None),
            P(),
            P("sp"),
            P("sp"),
            P(None, "sp"),
            P(None, "sp"),
            P(None, "sp"),
            P(None, "sp"),
            P(None, "sp"),
        ),
        out_specs=(P("mem", None, "sp"), P(), P()),
        check_vma=False,
    )
```

```python
import functools

import jax
import jax.numpy as jnp
from jax import lax
from jax.experimental import pallas as pl
from jax.experimental.pallas import tpu as pltpu
from jax.sharding import PartitionSpec as P

STEPS = 4
HALO = 2 * STEPS - 1
EARLY = 3
LANES = 128
GROUP = 4
PAIR = 4
SPAN = 4
NEAR = 4
VMEM_MODEL = 38 << 20
ROWS = 2

time_step = 1.0
coriolis = 0.1
perturb = 0.1


def in_hbm(array):
    return pltpu.with_memory_space_constraint(array, pltpu.HBM)


def ring(axis, step):
    count = lax.axis_size(axis)
    return [(i, (i + step) % count) for i in range(count)]


def prepare_kernel(place, weights, anom, *outs):
    *parts, partial = outs
    members, half = anom.shape[0], anom.shape[2] // 2
    chunks, width = partial.shape[0], partial.shape[3]
    first = place[0] * members
    scales = [weights[first + m] for m in range(members)]
    per = width // (SPAN * LANES)
    homes = [(part, r) for part in parts for r in range(part.shape[1])]

    def turn(homes, above):
        def columns(c, carry):
            swapped, totals = [], []
            for i in range(SPAN):
                block = anom[:, 0, pl.ds(above, half), pl.ds(pl.multiple_of((c * SPAN + i) * LANES, LANES), LANES)]
                swapped.append(jnp.swapaxes(block, 0, 1))
                total = scales[0] * block[0]
                for m in range(1, members):
                    total = total + scales[m] * block[m]
                totals.append(total)
            inner = pl.multiple_of(lax.rem(c, per) * (SPAN * LANES), SPAN * LANES)
            for i in range(SPAN):
                for r, (part, home) in enumerate(homes):
                    part[0, home, c * SPAN + i] = swapped[i][r]
                partial[lax.div(c, per), 0, pl.ds(above, half), pl.ds(inner + i * LANES, LANES)] = totals[i]
            return carry

        lax.fori_loop(0, chunks * per, columns, 0)

    for above in (0, half):
        turn(homes[above : above + half], above)


def prepare(place, weights, anomalies):
    members, fields, rows, columns = anomalies.shape
    chunks = NEAR
    width = columns // chunks
    smem = pl.BlockSpec(memory_space=pltpu.SMEM)
    tiles = columns // LANES
    late = HALO - EARLY
    parts = (EARLY, late, rows - 2 * HALO, EARLY, late)
    return pl.pallas_call(
        prepare_kernel,
        grid=(fields,),
        in_specs=[smem, smem, pl.BlockSpec((members, 1, rows, columns), lambda f: (0, f, 0, 0))],
        out_specs=[
            *(pl.BlockSpec((1, part, tiles, members, LANES), lambda f: (f, 0, 0, 0, 0)) for part in parts),
            pl.BlockSpec((chunks, 1, rows, width), lambda f: (0, f, 0, 0)),
        ],
        out_shape=[
            *(pltpu.HBM((fields, part, tiles, members, LANES), jnp.float32) for part in parts),
            jax.ShapeDtypeStruct((chunks, fields, rows, width), jnp.float32),
        ],
        compiler_params=pltpu.CompilerParams(vmem_limit_bytes=40 << 20),
        name="prepare",
    )(place, weights, anomalies)


def model_kernel(
    spots, lanes, low_c, centre, high_c, obs_weight, *refs
):
    *sources, out, state, heights, spare, sems = refs
    tall, tiles = state.shape[1], state.shape[2]
    rows = tall - 2 * HALO
    copies = []
    for f in range(3):
        row = 0
        for i, source in enumerate(sources):
            part = source.shape[1]
            copies.append(pltpu.make_async_copy(source.at[f], state.at[f, pl.ds(row, part)], sems.at[f, i]))
            row += part
    for copy in copies:
        copy.start()

    lane = lax.broadcasted_iota(jnp.int32, (8, LANES), 1)
    is_first = lane == 0
    is_last = lane == LANES - 1
    chunk_width = centre.shape[3]
    per = chunk_width // LANES

    edge = low_c.shape[2]

    def begin(f, i, carry):
        first = i * PAIR
        chunk = lax.div(first, per)
        inner = pl.multiple_of(lax.rem(first, per) * LANES, PAIR * LANES)
        for base, skip, at, count in (
            (low_c, edge - HALO, 0, HALO),
            (centre, 0, HALO, rows),
            (high_c, 0, HALO + rows, HALO),
        ):
            ready = []
            for r in range(count):
                for t in range(PAIR):
                    middle = base[chunk, f, pl.ds(skip + r, 1), pl.ds(inner + t * LANES, LANES)]
                    ready.append((r, t, middle + perturb * state[f, at + r, first + t]))
            for r, t, value in ready:
                state[f, at + r, first + t] = value
        return carry

    for f in range(3):
        for copy in copies[f * len(sources) : (f + 1) * len(sources)]:
            copy.wait()
        lax.fori_loop(0, tiles // PAIR, functools.partial(begin, f), 0)

    def memo(fetch):
        kept = {}

        def get(t):
            if isinstance(t, int):
                t %= tiles
            if t not in kept:
                kept[t] = fetch(t)
            return kept[t]

        return get

    def slope(piece):
        left = memo(lambda t: pltpu.roll(piece(t), LANES - 1, 1))
        right = memo(lambda t: pltpu.roll(piece(t), 1, 1))
        return lambda t: jnp.where(is_last, left(t + 1), left(t)) - jnp.where(is_first, right(t - 1), right(t))

    def rows_of(field, r):
        return memo(lambda key: field(r + key[0], key[1] % tiles))

    def in_row(get, i):
        return memo(lambda t: get((i, t)))

    def sweep(make, puts, r):
        for start in range(0, tiles, GROUP):
            span = range(start, start + GROUP)
            ready = [[make[i](t) for t in span] for i in range(len(make))]
            for i, values in enumerate(ready):
                for t, value in zip(span, values):
                    for put, part in zip(puts, value):
                        put(r + i, t, part)

    def height_rows(h, u, v, hn, r):
        gh, gu = rows_of(h, r), rows_of(u, r)
        flow = memo(lambda key: (1.0 + gh(key)) * gu(key))

        def row(i):
            across = slope(memo(lambda t: (1.0 + gh((i, t))) * v(r + i, t)))

            def value(t):
                along = flow((i + 1, t)) - flow((i - 1, t))
                return (gh((i, t)) - (0.5 * time_step) * (along + across(t)),)

            return value

        sweep([row(i) for i in range(2 * ROWS)], (hn,), r)

    def momentum_rows(h, u, v, un, vn, r):
        gh, gu, gv = rows_of(h, r), rows_of(u, r), rows_of(v, r)

        def row(i):
            slope_h, slope_u, slope_v = slope(in_row(gh, i)), slope(in_row(gu, i)), slope(in_row(gv, i))

            def value(t):
                cu, cv = gu((i, t)), gv((i, t))
                du = (gh((i + 1, t)) - gh((i - 1, t))) + cu * (gu((i + 1, t)) - gu((i - 1, t))) + cv * slope_u(t)
                dv = slope_h(t) + cu * (gv((i + 1, t)) - gv((i - 1, t))) + cv * slope_v(t)
                return (
                    cu + (time_step * coriolis) * cv - (0.5 * time_step) * du,
                    cv - (time_step * coriolis) * cu - (0.5 * time_step) * dv,
                )

            return value

        sweep([row(i) for i in range(ROWS)], (un, vn), r)

    def reader(ref, *lead):
        return lambda r, t: ref[(*lead, r, t)]

    def writer(ref, *lead):
        def put(r, t, value):
            ref[(*lead, r, t)] = value

        return put

    h = (state, 0)
    pairs = [((state, 1), (state, 2)), ((spare, 0), (spare, 1))]
    for step in range(STEPS):
        (u, v), (un, vn) = pairs[step % 2], pairs[1 - step % 2]
        low_row = 2 * step + 1
        fresh = (heights, step)

        def height_body(i, carry):
            height_rows(reader(*h), reader(*u), reader(*v), writer(*fresh), low_row + 2 * ROWS * i)
            return carry

        lax.fori_loop(0, (tall - 2 * low_row) // (2 * ROWS), height_body, 0)
        if step + 1 < STEPS:

            def momentum_body(i, carry):
                momentum_rows(reader(*fresh), reader(*u), reader(*v), writer(*un), writer(*vn), low_row + 1 + ROWS * i)
                return carry

            lax.fori_loop(0, (tall - 2 * low_row - 2) // ROWS, momentum_body, 0)
        h = fresh

    points, stations = spots.shape
    for group in range(stations // LANES):

        def pick(s, held):
            here = lane == s
            totals = [None] * STEPS
            for k in range(points):
                spot = spots[k, group * LANES + s]
                row, tile = HALO + lax.shift_right_logical(spot, tiles.bit_length() - 1), spot & (tiles - 1)
                factor = jnp.where(lane == lanes[k, group * LANES + s], obs_weight[k, group * LANES + s], 0.0)
                for step in range(STEPS):
                    value = factor * heights[step, row, tile]
                    totals[step] = value if totals[step] is None else totals[step] + value
            return tuple(
                jnp.where(here, jnp.sum(totals[step], axis=1, keepdims=True), held[step]) for step in range(STEPS)
            )

        zero = jnp.zeros((8, LANES), jnp.float32)
        held = lax.fori_loop(0, LANES, pick, (zero,) * STEPS, unroll=32)
        for step in range(STEPS):
            out[step, group] = held[step]


def run_model(spots, lanes, low_c, centre, high_c, obs_weight, *parts):
    fields, _, tiles, members, _ = parts[0].shape
    tall = sum(part.shape[1] for part in parts)
    smem = pl.BlockSpec(memory_space=pltpu.SMEM)
    vmem = pl.BlockSpec(memory_space=pltpu.VMEM)
    groups = obs_weight.shape[1] // LANES
    return pl.pallas_call(
        model_kernel,
        in_specs=[smem, smem, vmem, vmem, vmem, smem] + [pl.BlockSpec(memory_space=pl.ANY)] * len(parts),
        out_specs=vmem,
        out_shape=jax.ShapeDtypeStruct((STEPS, groups, members, LANES), jnp.float32),
        scratch_shapes=[
            pltpu.VMEM((fields, tall, tiles, members, LANES), jnp.float32),
            pltpu.VMEM((STEPS, tall, tiles, members, LANES), jnp.float32),
            pltpu.VMEM((2, tall, tiles, members, LANES), jnp.float32),
            pltpu.SemaphoreType.DMA((fields, len(parts))),
        ],
        compiler_params=pltpu.CompilerParams(vmem_limit_bytes=VMEM_MODEL),
        name="model",
    )(spots, lanes, low_c, centre, high_c, obs_weight, *parts)


def statistics_kernel(every, own, value, var, anom, packed):
    sources, steps, groups, members, _ = every.shape
    total = sources * members
    gram = jnp.zeros((total, total), jnp.float32)
    pull = jnp.zeros((1, total), jnp.float32)
    for step in range(steps):
        for group in range(groups):
            at = pl.ds(group * LANES, LANES)
            y = every[:, step, group].reshape(total, LANES)
            mean = jnp.sum(y, axis=0, keepdims=True) * (1.0 / total)
            anom[:, step, at] = (own[step, group] - mean) / perturb
            flat = (y - mean) / perturb
            weighted = flat * (1.0 / var[pl.ds(step, 1), at])
            innov = value[pl.ds(step, 1), at] - mean
            gram = gram + across(weighted, flat)
            pull = pull + across(innov, weighted)
    packed[pl.ds(0, total)] = gram
    packed[pl.ds(total, 8)] = jnp.broadcast_to(pull, (8, total))


def across(left, right):
    return lax.dot_general(
        left,
        right,
        (((1,), (1,)), ((), ())),
        precision=lax.Precision.HIGHEST,
        preferred_element_type=jnp.float32,
    )


def statistics(every, own, value, var):
    sources, steps, groups, members, _ = every.shape
    return pl.pallas_call(
        statistics_kernel,
        out_shape=[
            jax.ShapeDtypeStruct((members, steps, groups * LANES), jnp.float32),
            jax.ShapeDtypeStruct((sources * members + 8, sources * members), jnp.float32),
        ],
        name="statistics",
    )(every, own, value, var)


def body(
    anomalies,
    mean_state,
    weights,
    station_row,
    station_col,
    stencil_row,
    stencil_col,
    obs_weight,
    obs_value,
    obs_var,
):
    members, fields, rows, columns = anomalies.shape
    total = weights.shape[0]
    place = lax.axis_index("mem")
    count = lax.axis_size("mem")
    near = [[start + i for i in range(NEAR)] for start in range(0, count, NEAR)]
    width = columns // NEAR

    col = (station_col[None, :] + stencil_col) % columns
    spots = (station_row[None, :] + stencil_row) * (columns // LANES) + col // LANES
    lanes = col % LANES

    top, top_more, middle, bottom, bottom_more, partial_sum = prepare(place.reshape(1), in_hbm(weights), in_hbm(anomalies))
    own = [in_hbm(part) for part in (top, top_more, middle, bottom, bottom_more)]
    low = lax.ppermute(bottom, "sp", ring("sp", 1))
    high = lax.ppermute(top, "sp", ring("sp", -1))

    pieces = lax.all_to_all(partial_sum, "mem", 0, 0, axis_index_groups=near, tiled=True)
    piece = jnp.sum(pieces, axis=0)
    piece, low, high = lax.optimization_barrier((piece, low, high))
    hop = NEAR
    while hop < count:
        piece = piece + lax.ppermute(piece, "mem", [(i, i ^ hop) for i in range(count)])
        hop *= 2
    piece, top_more, bottom_more = lax.optimization_barrier((piece, top_more, bottom_more))
    low_more = lax.ppermute(bottom_more, "sp", ring("sp", 1))
    high_more = lax.ppermute(top_more, "sp", ring("sp", -1))
    piece = piece + lax.dynamic_slice_in_dim(mean_state, lax.rem(place, NEAR) * width, width, 2)
    centre = lax.all_to_all(
        jnp.broadcast_to(piece[None], (NEAR, *piece.shape)), "mem", 0, 0, axis_index_groups=near, tiled=True
    )
    edge = 8
    low_c = lax.ppermute(centre[:, :, rows - edge :], "sp", ring("sp", 1))
    high_c = lax.ppermute(centre[:, :, :edge], "sp", ring("sp", -1))

    seen = run_model(spots, lanes, low_c, centre, high_c, obs_weight, in_hbm(low), low_more, *own, in_hbm(high), high_more)
    every = lax.all_to_all(jnp.broadcast_to(seen[None], (count, *seen.shape)), "mem", 0, 0, tiled=True)
    obs_anom, packed = statistics(every, seen, obs_value, obs_var)
    count = lax.axis_size("sp")
    hop = 1
    while hop < count:
        packed = packed + lax.ppermute(packed, "sp", [(i, i ^ hop) for i in range(count)])
        hop *= 2
    hessian = packed[:total] + (total - 1) * jnp.eye(total, dtype=jnp.float32)
    gradient = (total - 1) * weights - packed[total]
    return (obs_anom, gradient, hessian)


def solution(mesh):
    return jax.shard_map(
        body,
        mesh=mesh,
        in_specs=(
            P("mem", None, "sp", None),
            P(None, "sp", None),
            P(),
            P("sp"),
            P("sp"),
            P(None, "sp"),
            P(None, "sp"),
            P(None, "sp"),
            P(None, "sp"),
            P(None, "sp"),
        ),
        out_specs=(P("mem", None, "sp"), P(), P()),
        check_vma=False,
    )
```
